32 devices in a mesh: dp: 2 (over x), row: 4 (over y, core), col: 4 (over z).
Axes of the slice: x: 2, y: 2, z: 4, core: 2. Of those that a mesh axis runs over, the one named last changes fastest.
Arguments:
- inputs: bfloat16 [4096, 576], P(('dp', 'col'), 'row'), may hold values from -10 to 10
- first_gain: float32 [576], P('row'), may hold values from 0.25 to 1.75
- query_weight: bfloat16 [576, 576], P('row', 'col'), may hold values from -0.25 to 0.25
- key_matrix: bfloat16 [576, 192], P('row', 'col'), may hold values from -0.25 to 0.25
- value_matrix: bfloat16 [576, 192], P('row', 'col'), may hold values from -0.25 to 0.25
- output_weight: bfloat16 [576, 576], P('col', 'row'), may hold values from -1.5 to 1.5
- second_gain: float32 [576], P('row'), may hold values from 0.25 to 1.75
- gate_weight: bfloat16 [576, 1536], P('row', 'col'), may hold values from -0.25 to 0.25
- up_weight: bfloat16 [576, 1536], P('row', 'col'), may hold values from -0.25 to 0.25
- down_weight: bfloat16 [1536, 576], P('col', 'row'), may hold values from -0.15625 to 0.15625
- cotangent: bfloat16 [4096, 576], P(('dp', 'col'), 'row'), may hold values from -6 to 6
Outputs:
- result: bfloat16 [4096, 576], P(('dp', 'col'), 'row')
- input_grad: bfloat16 [4096, 576], P(('dp', 'col'), 'row')
- first_gain_grad: float32 [576], P('row')
- query_grad: float32 [576, 576], P('row', 'col')
- key_grad: float32 [576, 192], P('row', 'col')
- value_grad: float32 [576, 192], P('row', 'col')
- output_grad: float32 [576, 576], P('col', 'row')
- second_gain_grad: float32 [576], P('row')
- gate_grad: float32 [576, 1536], P('row', 'col')
- up_grad: float32 [576, 1536], P('row', 'col')
- down_grad: float32 [1536, 576], P('col', 'row')
The draws below stay inside these ranges and needn't reach their ends.
All inputs are finite; a program needn't handle non-finite values.
Results may differ from the reference program's by a relative error of at most 0.035.
Values may be sent and summed in bfloat16 or wider, within the bound.
A program may use at most 64 MiB of HBM per device.

```python
import math
import jax
import jax.numpy as jnp
from jax import lax

MODEL_WIDTH = 576
QUERY_HEADS = 9
KEY_VALUE_HEADS = 3
HEAD_SIZE = 64
FF = 1536
SEQUENCE_LENGTH = 2048
TOKENS = 4096


def draw_inputs(key, part):
    key_cols = jax.random.fold_in(key, 11)
    key_body = jax.random.fold_in(key, 12)
    columns = jnp.arange(MODEL_WIDTH, dtype=jnp.float32)
    column_ramp = 0.7 * 3.0 ** (0.5 * columns / (MODEL_WIDTH - 1))
    column_jitter = jnp.exp(jax.random.uniform(key_cols, (MODEL_WIDTH,), jnp.float32, -0.3, 0.3))
    base_noise = jnp.clip(jax.random.normal(key_body, (TOKENS, MODEL_WIDTH), jnp.float32), -6.0, 6.0)
    return (base_noise * column_ramp * column_jitter).astype(jnp.bfloat16)


def block_scale(own_key, extent, shards, smallest, largest):
    def one(axis_at, blocks):
        steps = jax.random.uniform(jax.random.fold_in(jax.random.fold_in(own_key, 6), axis_at), (blocks,), jnp.float32, smallest / len(shards), largest / len(shards))
        return jnp.repeat(jnp.exp(steps), extent[axis_at] // blocks).reshape((-1,) + (1,) * (len(extent) - axis_at - 1))

    gain = one(*shards[0])
    for cut in shards[1:]:
        gain = gain * one(*cut)
    return gain


def scatter_about(stream_key, shape, deviation, bound, shards=(), kind=jnp.bfloat16):
    result = jax.random.normal(stream_key, shape, jnp.float32) * deviation
    if len(shards) > 0:
        result = block_scale(stream_key, shape, shards, -0.22, 0.18) * result
    return jnp.clip(result, min=-bound, max=bound).astype(kind)


def setup_inputs(seed: int = 0) -> dict:
    splits = jax.random.split(jax.random.key(seed), 12)
    return {
        "inputs": draw_inputs(jax.random.fold_in(splits[11], 71), 0),
        "first_gain": jnp.clip(1.0 + 0.15 * jax.random.normal(splits[1], (MODEL_WIDTH,), jnp.float32), 0.25, 1.75),
        "query_weight": scatter_about(splits[2], (MODEL_WIDTH, MODEL_WIDTH), MODEL_WIDTH ** -0.5, 0.25, ((0, 4), (1, 4))),
        "key_matrix": scatter_about(splits[3], (MODEL_WIDTH, KEY_VALUE_HEADS * HEAD_SIZE), MODEL_WIDTH ** -0.5, 0.25, ((0, 4), (1, 4))),
        "value_matrix": scatter_about(splits[4], (MODEL_WIDTH, KEY_VALUE_HEADS * HEAD_SIZE), MODEL_WIDTH ** -0.5, 0.25, ((0, 4), (1, 4))),
        "output_weight": scatter_about(splits[5], (MODEL_WIDTH, MODEL_WIDTH), 16 ** -0.5, 1.5, ((0, 4), (1, 4))),
        "second_gain": jnp.clip(1.0 + 0.15 * jax.random.normal(splits[6], (MODEL_WIDTH,), jnp.float32), 0.25, 1.75),
        "gate_weight": scatter_about(splits[7], (MODEL_WIDTH, FF), MODEL_WIDTH ** -0.5, 0.25, ((0, 4), (1, 4))),
        "up_weight": scatter_about(splits[8], (MODEL_WIDTH, FF), MODEL_WIDTH ** -0.5, 0.25, ((0, 4), (1, 4))),
        "down_weight": scatter_about(splits[9], (FF, MODEL_WIDTH), FF ** -0.5, 0.15625, ((0, 4), (1, 4))),
        "cotangent": scatter_about(splits[10], (TOKENS, MODEL_WIDTH), 1.0, 6.0, ((0, 8), (1, 4))),
    }


EPS = 1e-05
THETA = 100000.0
NEGATIVE_FILL = -1e+30

@jax.custom_vjp
def low(v):
    return lax.optimization_barrier(v.astype(jnp.bfloat16)).astype(jnp.float32)

@jax.custom_vjp
def low_back(v):
    return v

def low_keep(v):
    return (low(v), None)

def low_pass(kept, grad):
    return (grad,)

def back_keep(v):
    return (v, None)

def back_low(kept, grad):
    return (low(grad),)
low.defvjp(low_keep, low_pass)
low_back.defvjp(back_keep, back_low)

def matmul(left, right):
    return jnp.dot(left, right, precision=lax.Precision.HIGHEST, preferred_element_type=jnp.float32)

def rotate(values, positions, first_col, direction):
    row_total = values.shape[0]
    col_total = values.shape[1]
    pair_cols = first_col + 2 * jnp.arange(col_total // 2)
    pair_index = (pair_cols % HEAD_SIZE // 2).astype(jnp.float32)
    inverse = 1.0 / THETA ** (2.0 * pair_index / HEAD_SIZE)
    angles = positions.astype(jnp.float32)[:, None] * inverse[None, :]
    cosine = jnp.cos(angles)
    sine_part = jnp.sin(angles)
    pair_view = values.reshape(row_total, col_total // 2, 2)
    even_part = pair_view[:, :, 0]
    odd_part = pair_view[:, :, 1]
    turned = jnp.stack([even_part * cosine - direction * odd_part * sine_part, direction * even_part * sine_part + odd_part * cosine], axis=2)
    return turned.reshape(row_total, col_total)

def rms_norm(source, norm_gain):
    norm_scale = lax.rsqrt(lax.optimization_barrier(jnp.mean(source * source, axis=1, keepdims=True)) + EPS)
    return source * norm_scale * norm_gain

def attention(queries, rows_of_key, rows_of_value):
    rows_in_block = min(512, SEQUENCE_LENGTH)
    query_groups = QUERY_HEADS // KEY_VALUE_HEADS
    soft_scale = 1.0 / math.sqrt(HEAD_SIZE)
    heads_of_key = rows_of_key.reshape(SEQUENCE_LENGTH, KEY_VALUE_HEADS, HEAD_SIZE)
    heads_of_value = rows_of_value.reshape(SEQUENCE_LENGTH, KEY_VALUE_HEADS, HEAD_SIZE)

    def one_block(seq_item):
        queries_block_slice, block_first = seq_item
        per_head_view = queries_block_slice.reshape(rows_in_block, KEY_VALUE_HEADS, query_groups, HEAD_SIZE)
        raw_scores = low_back(jnp.einsum('ngjd,mgd->gjnm', per_head_view, heads_of_key, precision=lax.Precision.HIGHEST))
        scores = raw_scores * soft_scale
        allowed = jnp.arange(SEQUENCE_LENGTH)[None, :] <= (block_first + jnp.arange(rows_in_block))[:, None]
        masked = jnp.where(allowed, scores, NEGATIVE_FILL)
        log_total = jax.nn.logsumexp(masked, axis=3, keepdims=True)
        probs = jnp.where(allowed, jnp.exp(masked - log_total), 0.0)
        attended = jnp.einsum('gjnm,mgd->ngjd', low(probs), heads_of_value, precision=lax.Precision.HIGHEST)
        return attended.reshape(rows_in_block, QUERY_HEADS * HEAD_SIZE)
    query_blocks = queries.reshape(SEQUENCE_LENGTH // rows_in_block, rows_in_block, QUERY_HEADS * HEAD_SIZE)
    block_firsts = jnp.arange(SEQUENCE_LENGTH // rows_in_block, dtype=jnp.int32) * rows_in_block
    outputs = lax.map(jax.checkpoint(one_block), (query_blocks, block_firsts))
    return outputs.reshape(SEQUENCE_LENGTH, QUERY_HEADS * HEAD_SIZE)

def layer(source, first_gain, query_weight, key_matrix, value_matrix, output_weight, second_gain, gate_weight, up_weight, down_weight):
    positions = jnp.arange(SEQUENCE_LENGTH)
    normed = low(rms_norm(source, first_gain))
    queries = low(rotate(low_back(matmul(normed, query_weight)), positions, 0, 1.0))
    rows_of_key = low(rotate(low_back(matmul(normed, key_matrix)), positions, 0, 1.0))
    rows_of_value = low(low_back(matmul(normed, value_matrix)))
    attended = low(low_back(attention(queries, rows_of_key, rows_of_value)))
    middle = source + low_back(matmul(attended, output_weight))
    second_normed = low(rms_norm(middle, second_gain))
    gate_values = low_back(matmul(second_normed, gate_weight))
    up_values = low_back(matmul(second_normed, up_weight))
    active = low(jax.nn.silu(gate_values) * up_values)
    return middle + matmul(active, down_weight)

def reference(inputs, first_gain, query_weight, key_matrix, value_matrix, output_weight, second_gain, gate_weight, up_weight, down_weight, cotangent):
    params = tuple((weight_item.astype(jnp.float32) for weight_item in (first_gain, query_weight, key_matrix, value_matrix, output_weight, second_gain, gate_weight, up_weight, down_weight)))
    seq_count = TOKENS // SEQUENCE_LENGTH
    sources = inputs.astype(jnp.float32).reshape(seq_count, SEQUENCE_LENGTH, MODEL_WIDTH)
    upstreams = cotangent.astype(jnp.float32).reshape(seq_count, SEQUENCE_LENGTH, MODEL_WIDTH)

    def per_sequence(totals, seq_item):
        source, upstream = seq_item
        output_rows, pull_back = jax.vjp(layer, source, *params)
        gradients = pull_back(upstream)
        totals = tuple((running + addend for running, addend in zip(totals, gradients[1:])))
        return (totals, (output_rows.astype(jnp.bfloat16), gradients[0].astype(jnp.bfloat16)))
    zero_filled = tuple((jnp.zeros(param_item.shape, jnp.float32) for param_item in params))
    totals, outputs = lax.scan(per_sequence, zero_filled, (sources, upstreams))
    return (outputs[0].reshape(TOKENS, MODEL_WIDTH), outputs[1].reshape(TOKENS, MODEL_WIDTH), totals[0], totals[1], totals[2], totals[3], totals[4], totals[5], totals[6], totals[7], totals[8])
```

```python
import functools
import math

import jax
import jax.numpy as jnp
from jax import lax
from jax.experimental import pallas as pl
from jax.experimental.pallas import tpu as pltpu
from jax.sharding import PartitionSpec as P

QUERY_HEADS = 9
KEY_VALUE_HEADS = 3
HEAD_SIZE = 64
SEQUENCE_LENGTH = 2048
EPS = 1e-05
THETA = 100000.0
NEGATIVE_FILL = -1e30
MESH = pl.DeviceIdType.MESH
BF = jnp.bfloat16
F32 = jnp.float32


def exchange_kernel(plan, axes, *refs):
    count = len(plan)
    ins, outs = refs[:count], refs[count : 2 * count]
    send_sem, recv_sem, local_sem = refs[2 * count :]
    barrier = pltpu.get_barrier_semaphore()
    total = 0
    for axis, size in axes:
        me = lax.axis_index(axis)
        for step in range(1, size):
            pl.semaphore_signal(
                barrier, inc=1, device_id={axis: lax.rem(me + step, size)}, device_id_type=MESH
            )
        total += size - 1
    pl.semaphore_wait(barrier, total)
    sizes = dict(axes)
    copies = []
    for item, (axis, mode) in enumerate(plan):
        size = sizes[axis]
        me = lax.axis_index(axis)
        for step in range(1, size):
            peer = lax.rem(me + step, size)
            source = ins[item] if mode == "g" else ins[item].at[peer]
            copy = pltpu.make_async_remote_copy(
                src_ref=source,
                dst_ref=outs[item].at[me],
                send_sem=send_sem.at[item, step],
                recv_sem=recv_sem.at[item, step],
                device_id={axis: peer},
                device_id_type=MESH,
            )
            copy.start()
            copies.append(copy)
    for item, (axis, mode) in enumerate(plan):
        me = lax.axis_index(axis)
        source = ins[item] if mode == "g" else ins[item].at[me]
        copy = pltpu.make_async_copy(source, outs[item].at[me], local_sem.at[item])
        copy.start()
        copies.append(copy)
    for copy in copies:
        copy.wait()


def exchange(ident, *items):
    plan = tuple((axis, mode) for _, axis, mode in items)
    axes = tuple((axis, lax.axis_size(axis)) for axis in dict.fromkeys(a for a, _ in plan))
    arrays = [array for array, _, _ in items]
    widest = max(size for _, size in axes)
    out_shape = tuple(
        jax.ShapeDtypeStruct(
            ((lax.axis_size(axis),) + array.shape) if mode == "g" else array.shape, array.dtype
        )
        for array, axis, mode in items
    )
    spec = pl.BlockSpec(memory_space=pltpu.VMEM)
    return pl.pallas_call(
        functools.partial(exchange_kernel, plan, axes),
        out_shape=out_shape,
        in_specs=[spec] * len(arrays),
        out_specs=tuple([spec] * len(arrays)),
        scratch_shapes=[
            pltpu.SemaphoreType.DMA((len(arrays), widest)),
            pltpu.SemaphoreType.DMA((len(arrays), widest)),
            pltpu.SemaphoreType.DMA((len(arrays),)),
        ],
        compiler_params=pltpu.CompilerParams(
            collective_id=ident, has_side_effects=True
        ),
        name="exchange_%d" % ident,
    )(*arrays)


def dot(left, right, left_dim=1, right_dim=0):
    return lax.dot_general(
        left, right, (((left_dim,), (right_dim,)), ((), ())), preferred_element_type=F32
    )


def rotate(values, cosine, sine):
    repeats = values.shape[1] // HEAD_SIZE
    cosine = jnp.tile(cosine, (1, repeats))
    sine = jnp.tile(sine, (1, repeats))
    even = (jnp.arange(values.shape[1]) % 2 == 0)[None, :]
    partner = jnp.where(even, -jnp.roll(values, -1, axis=1), jnp.roll(values, 1, axis=1))
    return values * cosine + partner * sine


def group_split(values):
    rows = values.shape[0]
    per = values.shape[1] // (KEY_VALUE_HEADS * HEAD_SIZE)
    shaped = values.reshape(rows, KEY_VALUE_HEADS, per, HEAD_SIZE).transpose(1, 2, 0, 3)
    return shaped.reshape(KEY_VALUE_HEADS, per * rows, HEAD_SIZE)


def group_merge(values, rows):
    per = values.shape[1] // rows
    shaped = values.reshape(KEY_VALUE_HEADS, per, rows, HEAD_SIZE).transpose(2, 0, 1, 3)
    return shaped.reshape(rows, KEY_VALUE_HEADS * per * HEAD_SIZE)


def norm_scale(source):
    return lax.rsqrt(jnp.mean(source * source, axis=1, keepdims=True) + EPS)


def norm_back(source, scale, gain, upstream):
    inner = jnp.sum(upstream * gain * source, axis=1, keepdims=True)
    cubed = scale * scale * scale
    d_source = scale * gain * upstream - source * cubed * inner / source.shape[1]
    return d_source, jnp.sum(upstream * source * scale, axis=0)


def on_device(
    inputs,
    first_gain,
    query_weight,
    key_matrix,
    value_matrix,
    output_weight,
    second_gain,
    gate_weight,
    up_weight,
    down_weight,
    cotangent,
):
    rows = lax.axis_size("row")
    cols = lax.axis_size("col")
    block_tokens, feat = inputs.shape
    tokens = block_tokens // rows
    width = feat * rows
    hidden = gate_weight.shape[1]
    q_cols = query_weight.shape[1]
    k_cols = key_matrix.shape[1]
    row_index = lax.axis_index("row")
    col_index = lax.axis_index("col")
    soft_scale = 1.0 / math.sqrt(HEAD_SIZE)

    ffn_block = jnp.concatenate([gate_weight, up_weight, down_weight.T], axis=1)
    qo_block = jnp.concatenate([query_weight, key_matrix, value_matrix, output_weight.T], axis=1)
    joint = jnp.concatenate([inputs, cotangent], axis=1).reshape(rows, tokens, 2 * feat)
    gains = jnp.stack([first_gain, second_gain])
    joint_all, gain_all, ffn_all, qo_cols = exchange(
        0,
        (joint, "row", "s"),
        (gains, "row", "g"),
        (ffn_block, "row", "g"),
        (qo_block, "col", "g"),
    )
    joint_all = joint_all.transpose(1, 0, 2)
    source = joint_all[:, :, :feat].reshape(tokens, width).astype(F32)
    cot_low = joint_all[:, :, feat:].reshape(tokens, width)
    upstream = cot_low.astype(F32)
    gain_all = gain_all.transpose(1, 0, 2).reshape(2, width)
    gain1, gain2 = gain_all[0:1], gain_all[1:2]
    first_scale = norm_scale(source)
    normed1 = (source * first_scale * gain1).astype(BF)

    qo_all, cot_all = exchange(1, (qo_cols, "row", "g"), (cot_low, "col", "g"))
    qo_all = qo_all.transpose(0, 2, 1, 3).reshape(width, cols, q_cols * 2 + 2 * k_cols)
    at = 0
    parts = []
    for size in (q_cols, k_cols, k_cols, q_cols):
        parts.append(qo_all[:, :, at : at + size].reshape(width, cols * size))
        at += size
    qkv_weight = jnp.concatenate(parts[:3], axis=1)
    out_t = parts[3]
    kv_width = cols * k_cols

    first_pos = (col_index * block_tokens + row_index * tokens) % SEQUENCE_LENGTH
    positions = (first_pos + jnp.arange(tokens)).astype(F32)
    pair_index = (jnp.arange(HEAD_SIZE) // 2).astype(F32)
    inverse = 1.0 / THETA ** (2.0 * pair_index / HEAD_SIZE)
    angles = positions[:, None] * inverse[None, :]
    cosine, sine = jnp.cos(angles), jnp.sin(angles)

    qkv = dot(normed1, qkv_weight)
    turned = rotate(qkv[:, : width + kv_width], cosine, sine)
    queries = turned[:, :width].astype(BF)
    kv_low = jnp.concatenate([turned[:, width:], qkv[:, width + kv_width :]], axis=1).astype(BF)
    (kv_cols,) = exchange(2, (kv_low, "col", "g"))
    (kv_all,) = exchange(3, (kv_cols, "row", "g"))
    kv_all = kv_all.reshape(rows * cols * tokens, 2, KEY_VALUE_HEADS, HEAD_SIZE)
    keys = kv_all[:, 0].transpose(1, 0, 2)
    values = kv_all[:, 1].transpose(1, 0, 2)
    key_index = jnp.arange(rows * cols * tokens)
    key_row = key_index // (cols * tokens)
    key_col = key_index // tokens % cols
    key_global = key_col * block_tokens + key_row * tokens + key_index % tokens
    query_global = col_index * block_tokens + row_index * tokens + jnp.arange(tokens)
    query_global = jnp.tile(query_global, QUERY_HEADS // KEY_VALUE_HEADS)
    allowed = (key_global[None, :] <= query_global[:, None]) & (
        key_global[None, :] // SEQUENCE_LENGTH == query_global[:, None] // SEQUENCE_LENGTH
    )
    split_q = group_split(queries)
    scores = jnp.einsum("gqd,gkd->gqk", split_q, keys, preferred_element_type=F32) * soft_scale
    masked = jnp.where(allowed[None], scores, NEGATIVE_FILL)
    top = jnp.max(masked, axis=2, keepdims=True)
    terms = jnp.exp(masked - top)
    total = jnp.sum(terms, axis=2, keepdims=True)
    probs = terms / total
    probs_low = probs.astype(BF)
    att_split = jnp.einsum("gqk,gkd->gqd", probs_low, values, preferred_element_type=F32)
    attended = group_merge(att_split, tokens).astype(BF)
    middle = source + dot(attended, out_t, 1, 1)
    second_scale = norm_scale(middle)
    normed2 = (middle * second_scale * gain2).astype(BF)

    (normed2_all,) = exchange(4, (normed2, "col", "g"))
    normed2_all = normed2_all.reshape(cols * tokens, width)
    cot_all = cot_all.reshape(cols * tokens, width)
    ffn_all = ffn_all.reshape(width, 3 * hidden)
    gate_up = dot(normed2_all, ffn_all[:, : 2 * hidden])
    gate, up = gate_up[:, :hidden], gate_up[:, hidden:]
    down_t = ffn_all[:, 2 * hidden :]
    sigma = jax.nn.sigmoid(gate)
    active = (gate * sigma * up).astype(BF)
    d_active = dot(cot_all, down_t)
    d_gate = (d_active * up * sigma * (1.0 + gate * (1.0 - sigma))).astype(BF)
    d_up = (d_active * gate * sigma).astype(BF)
    d_gate_up = jnp.concatenate([d_gate, d_up], axis=1)
    d_second_part = dot(d_gate_up, ffn_all[:, : 2 * hidden], 1, 1).astype(BF)
    ffn_part = dot(active, down_t, 1, 1).astype(BF)
    d_second, ffn_out = exchange(
        5,
        (d_second_part.reshape(cols, tokens, width), "col", "s"),
        (ffn_part.reshape(cols, tokens, width), "col", "s"),
    )
    d_second = jnp.sum(d_second.astype(F32), axis=0)
    result = middle + jnp.sum(ffn_out.astype(F32), axis=0)
    ffn_grad = jnp.concatenate(
        [dot(normed2_all, d_gate_up, 0, 0), dot(cot_all, active, 0, 0)], axis=1
    ).astype(BF)

    second_back, gain2_grad = norm_back(middle, second_scale, gain2, d_second)
    d_middle = upstream + second_back
    d_attn = d_middle.astype(BF)
    d_attended = dot(d_attn, out_t).astype(BF)
    out_grad = dot(d_attn, attended, 0, 0)
    d_split = group_split(d_attended)
    row_dots = jnp.sum(d_split.astype(F32) * att_split, axis=2, keepdims=True)
    d_probs = jnp.einsum("gqd,gkd->gqk", d_split, values, preferred_element_type=F32)
    d_raw = (probs * (d_probs - row_dots) * soft_scale).astype(BF)
    d_query = group_merge(
        jnp.einsum("gqk,gkd->gqd", d_raw, keys, preferred_element_type=F32), tokens
    )
    d_key = jnp.einsum("gqk,gqd->kgd", d_raw, split_q, preferred_element_type=F32)
    d_value = jnp.einsum("gqk,gqd->kgd", probs_low, d_split, preferred_element_type=F32)
    d_kv = jnp.stack([d_key, d_value], axis=1).astype(BF)
    d_kv = d_kv.reshape(rows, cols * tokens, 2 * kv_width)
    d_kv_rows, ffn_rows = exchange(
        6, (d_kv, "row", "s"), (ffn_grad.reshape(rows, feat, 3 * hidden), "row", "s")
    )
    d_kv_sum = jnp.sum(d_kv_rows.astype(F32), axis=0).astype(BF)
    ffn_sum = jnp.sum(ffn_rows.astype(F32), axis=0).astype(BF)
    d_kv_cols, ffn_dp = exchange(
        7, (d_kv_sum.reshape(cols, tokens, 2 * kv_width), "col", "s"), (ffn_sum, "dp", "g")
    )
    d_kv_own = jnp.sum(d_kv_cols.astype(F32), axis=0)
    d_turned = rotate(jnp.concatenate([d_query, d_kv_own[:, :kv_width]], axis=1), cosine, -sine)
    d_qkv = jnp.concatenate([d_turned, d_kv_own[:, kv_width:]], axis=1).astype(BF)
    d_first = dot(d_qkv, qkv_weight, 1, 1)
    qkv_grad = dot(normed1, d_qkv, 0, 0)
    first_back, gain1_grad = norm_back(source, first_scale, gain1, d_first)
    input_grad_own = (d_middle + first_back).astype(BF)

    def by_col(grad):
        return grad.reshape(width, cols, grad.shape[1] // cols)

    qo_grad = jnp.concatenate(
        [
            by_col(qkv_grad[:, :width]),
            by_col(qkv_grad[:, width : width + kv_width]),
            by_col(qkv_grad[:, width + kv_width :]),
            by_col(out_grad),
        ],
        axis=2,
    ).astype(BF)
    qo_grad = qo_grad.reshape(rows, feat, cols, -1).transpose(0, 2, 1, 3)
    gain_grads = jnp.stack([gain1_grad, gain2_grad]).reshape(2, rows, feat).transpose(1, 0, 2)
    results = jnp.stack([result.astype(BF), input_grad_own])
    results = results.reshape(2, tokens, rows, feat).transpose(2, 1, 0, 3)
    results = results.reshape(rows, tokens, 2 * feat)
    qo_rows, gain_rows, result_rows = exchange(
        8, (qo_grad, "row", "s"), (gain_grads, "row", "s"), (results, "row", "s")
    )
    qo_sum = jnp.sum(qo_rows.astype(F32), axis=0).astype(BF)
    qo_cols_grad, gain_cols = exchange(
        9, (qo_sum, "col", "s"), (jnp.sum(gain_rows, axis=0), "col", "g")
    )
    qo_own = jnp.sum(qo_cols_grad.astype(F32), axis=0).astype(BF)
    qo_dp, gain_dp = exchange(10, (qo_own, "dp", "g"), (jnp.sum(gain_cols, axis=0), "dp", "g"))
    qo_final = jnp.sum(qo_dp.astype(F32), axis=0)
    ffn_final = jnp.sum(ffn_dp.astype(F32), axis=0)
    gain_final = jnp.sum(gain_dp, axis=0)
    result_rows = result_rows.reshape(block_tokens, 2 * feat)
    return (
        result_rows[:, :feat],
        result_rows[:, feat:],
        gain_final[0],
        qo_final[:, :q_cols],
        qo_final[:, q_cols : q_cols + k_cols],
        qo_final[:, q_cols + k_cols : q_cols + 2 * k_cols],
        qo_final[:, q_cols + 2 * k_cols :].T,
        gain_final[1],
        ffn_final[:, :hidden],
        ffn_final[:, hidden : 2 * hidden],
        ffn_final[:, 2 * hidden :].T,
    )


def solution(mesh):
    placed = (
        P(("dp", "col"), "row"),
        P("row"),
        P("row", "col"),
        P("row", "col"),
        P("row", "col"),
        P("col", "row"),
        P("row"),
        P("row", "col"),
        P("row", "col"),
        P("col", "row"),
        P(("dp", "col"), "row"),
    )
    return jax.shard_map(
        on_device,
        mesh=mesh,
        in_specs=placed,
        out_specs=(
            P(("dp", "col"), "row"),
            P(("dp", "col"), "row"),
            P("row"),
            P("row", "col"),
            P("row", "col"),
            P("row", "col"),
            P("col", "row"),
            P("row"),
            P("row", "col"),
            P("row", "col"),
            P("col", "row"),
        ),
        check_vma=False,
    )
```

```python
import functools
import math

import jax
import jax.numpy as jnp
from jax import lax
from jax.experimental import pallas as pl
from jax.experimental.pallas import tpu as pltpu
from jax.sharding import PartitionSpec as P

QUERY_HEADS = 9
KEY_VALUE_HEADS = 3
HEAD_SIZE = 64
SEQUENCE_LENGTH = 2048
EPS = 1e-05
THETA = 100000.0
NEGATIVE_FILL = -1e30
MESH = pl.DeviceIdType.MESH
BF = jnp.bfloat16
F32 = jnp.float32


def exchange_kernel(plan, axes, *refs):
    count = len(plan)
    ins, outs = refs[:count], refs[count : 2 * count]
    send_sem, recv_sem, local_sem = refs[2 * count :]
    barrier = pltpu.get_barrier_semaphore()
    total = 0
    for axis, size in axes:
        me = lax.axis_index(axis)
        for step in range(1, size):
            pl.semaphore_signal(
                barrier, inc=1, device_id={axis: lax.rem(me + step, size)}, device_id_type=MESH
            )
        total += size - 1
    pl.semaphore_wait(barrier, total)
    sizes = dict(axes)
    copies = []
    relays = []
    for item, (axis, mode) in enumerate(plan):
        size = sizes[axis]
        me = lax.axis_index(axis)
        near = me + 1 - 2 * lax.rem(me, 2)
        for step in range(1, size):
            peer = lax.rem(me + step, size)
            if mode == "r":
                if step == 3:
                    continue
                peer = near if step == 1 else lax.rem(me + 2, size)
            source = ins[item].at[peer] if mode == "s" else ins[item]
            copy = pltpu.make_async_remote_copy(
                src_ref=source,
                dst_ref=outs[item].at[me],
                send_sem=send_sem.at[item, step],
                recv_sem=recv_sem.at[item, step],
                device_id={axis: peer},
                device_id_type=MESH,
            )
            copy.start()
            if mode == "r" and step == 2:
                relays.append((item, axis, peer, near, copy))
            else:
                copies.append(copy)
    for item, (axis, mode) in enumerate(plan):
        me = lax.axis_index(axis)
        source = ins[item].at[me] if mode == "s" else ins[item]
        copy = pltpu.make_async_copy(source, outs[item].at[me], local_sem.at[item])
        copy.start()
        copies.append(copy)
    for item, axis, across, near, arrived in relays:
        arrived.wait_recv()
        copy = pltpu.make_async_remote_copy(
            src_ref=outs[item].at[across],
            dst_ref=outs[item].at[across],
            send_sem=send_sem.at[item, 3],
            recv_sem=recv_sem.at[item, 3],
            device_id={axis: near},
            device_id_type=MESH,
        )
        copy.start()
        copies.append(copy)
    for _, _, _, _, arrived in relays:
        arrived.wait_send()
    for copy in copies:
        copy.wait()


def exchange(ident, *items):
    items = [
        (array, axis, "r" if mode == "g" and axis == "row" and lax.axis_size(axis) == 4 else mode)
        for array, axis, mode in items
    ]
    plan = tuple((axis, mode) for _, axis, mode in items)
    axes = tuple((axis, lax.axis_size(axis)) for axis in dict.fromkeys(a for a, _ in plan))
    arrays = [array for array, _, _ in items]
    widest = max(size for _, size in axes)
    out_shape = tuple(
        jax.ShapeDtypeStruct(
            array.shape if mode == "s" else ((lax.axis_size(axis),) + array.shape), array.dtype
        )
        for array, axis, mode in items
    )
    spec = pl.BlockSpec(memory_space=pltpu.VMEM)
    return pl.pallas_call(
        functools.partial(exchange_kernel, plan, axes),
        out_shape=out_shape,
        in_specs=[spec] * len(arrays),
        out_specs=tuple([spec] * len(arrays)),
        scratch_shapes=[
            pltpu.SemaphoreType.DMA((len(arrays), widest)),
            pltpu.SemaphoreType.DMA((len(arrays), widest)),
            pltpu.SemaphoreType.DMA((len(arrays),)),
        ],
        compiler_params=pltpu.CompilerParams(
            collective_id=ident, has_side_effects=True
        ),
        name="exchange_%d" % ident,
    )(*arrays)


def dot(left, right, left_dim=1, right_dim=0):
    return lax.dot_general(
        left, right, (((left_dim,), (right_dim,)), ((), ())), preferred_element_type=F32
    )


def rotate(values, cosine, sine):
    repeats = values.shape[1] // HEAD_SIZE
    cosine = jnp.tile(cosine, (1, repeats))
    sine = jnp.tile(sine, (1, repeats))
    even = (jnp.arange(values.shape[1]) % 2 == 0)[None, :]
    partner = jnp.where(even, -jnp.roll(values, -1, axis=1), jnp.roll(values, 1, axis=1))
    return values * cosine + partner * sine


def group_split(values):
    rows = values.shape[0]
    per = values.shape[1] // (KEY_VALUE_HEADS * HEAD_SIZE)
    shaped = values.reshape(rows, KEY_VALUE_HEADS, per, HEAD_SIZE).transpose(1, 2, 0, 3)
    return shaped.reshape(KEY_VALUE_HEADS, per * rows, HEAD_SIZE)


def group_merge(values, rows):
    per = values.shape[1] // rows
    shaped = values.reshape(KEY_VALUE_HEADS, per, rows, HEAD_SIZE).transpose(2, 0, 1, 3)
    return shaped.reshape(rows, KEY_VALUE_HEADS * per * HEAD_SIZE)


def norm_scale(source):
    return lax.rsqrt(jnp.mean(source * source, axis=1, keepdims=True) + EPS)


def norm_back(source, scale, gain, upstream):
    inner = jnp.sum(upstream * gain * source, axis=1, keepdims=True)
    cubed = scale * scale * scale
    d_source = scale * gain * upstream - source * cubed * inner / source.shape[1]
    return d_source, jnp.sum(upstream * source * scale, axis=0)


def on_device(
    inputs,
    first_gain,
    query_weight,
    key_matrix,
    value_matrix,
    output_weight,
    second_gain,
    gate_weight,
    up_weight,
    down_weight,
    cotangent,
):
    rows = lax.axis_size("row")
    cols = lax.axis_size("col")
    block_tokens, feat = inputs.shape
    tokens = block_tokens // rows
    width = feat * rows
    hidden = gate_weight.shape[1]
    q_cols = query_weight.shape[1]
    k_cols = key_matrix.shape[1]
    row_index = lax.axis_index("row")
    col_index = lax.axis_index("col")
    soft_scale = 1.0 / math.sqrt(HEAD_SIZE)

    ffn_block = jnp.concatenate([gate_weight, up_weight, down_weight.T], axis=1)
    qo_block = jnp.concatenate([query_weight, key_matrix, value_matrix, output_weight.T], axis=1)
    joint = jnp.concatenate([inputs, cotangent], axis=1).reshape(rows, tokens, 2 * feat)
    gains = jnp.stack([first_gain, second_gain])
    joint_all, gain_all, qo_cols = exchange(
        0, (joint, "row", "s"), (gains, "row", "g"), (qo_block, "col", "g")
    )
    joint_all = joint_all.transpose(1, 0, 2)
    source = joint_all[:, :, :feat].reshape(tokens, width).astype(F32)
    cot_low = joint_all[:, :, feat:].reshape(tokens, width)
    upstream = cot_low.astype(F32)
    gain_all = gain_all.transpose(1, 0, 2).reshape(2, width)
    gain1, gain2 = gain_all[0:1], gain_all[1:2]
    first_scale = norm_scale(source)
    normed1 = (source * first_scale * gain1).astype(BF)

    qo_all, cot_all = exchange(1, (qo_cols, "row", "g"), (cot_low, "col", "g"))
    qo_all = qo_all.transpose(0, 2, 1, 3).reshape(width, cols, q_cols * 2 + 2 * k_cols)
    at = 0
    parts = []
    for size in (q_cols, k_cols, k_cols, q_cols):
        parts.append(qo_all[:, :, at : at + size].reshape(width, cols * size))
        at += size
    qkv_weight = jnp.concatenate(parts[:3], axis=1)
    out_t = parts[3]
    kv_width = cols * k_cols

    first_pos = (col_index * block_tokens + row_index * tokens) % SEQUENCE_LENGTH
    positions = (first_pos + jnp.arange(tokens)).astype(F32)
    pair_index = (jnp.arange(HEAD_SIZE) // 2).astype(F32)
    inverse = 1.0 / THETA ** (2.0 * pair_index / HEAD_SIZE)
    angles = positions[:, None] * inverse[None, :]
    cosine, sine = jnp.cos(angles), jnp.sin(angles)

    qkv = dot(normed1, qkv_weight)
    turned = rotate(qkv[:, : width + kv_width], cosine, sine)
    queries = turned[:, :width].astype(BF)
    kv_low = jnp.concatenate([turned[:, width:], qkv[:, width + kv_width :]], axis=1).astype(BF)
    (kv_cols,) = exchange(2, (kv_low, "col", "g"))
    (kv_all,) = exchange(3, (kv_cols, "row", "g"))
    kv_all = kv_all.reshape(rows * cols * tokens, 2, KEY_VALUE_HEADS, HEAD_SIZE)
    keys = kv_all[:, 0].transpose(1, 0, 2)
    values = kv_all[:, 1].transpose(1, 0, 2)
    key_index = jnp.arange(rows * cols * tokens)
    key_row = key_index // (cols * tokens)
    key_col = key_index // tokens % cols
    key_global = key_col * block_tokens + key_row * tokens + key_index % tokens
    query_global = col_index * block_tokens + row_index * tokens + jnp.arange(tokens)
    query_global = jnp.tile(query_global, QUERY_HEADS // KEY_VALUE_HEADS)
    allowed = (key_global[None, :] <= query_global[:, None]) & (
        key_global[None, :] // SEQUENCE_LENGTH == query_global[:, None] // SEQUENCE_LENGTH
    )
    split_q = group_split(queries)
    scores = jnp.einsum("gqd,gkd->gqk", split_q, keys, preferred_element_type=F32) * soft_scale
    masked = jnp.where(allowed[None], scores, NEGATIVE_FILL)
    top = jnp.max(masked, axis=2, keepdims=True)
    terms = jnp.exp(masked - top)
    total = jnp.sum(terms, axis=2, keepdims=True)
    probs = terms / total
    probs_low = probs.astype(BF)
    att_split = jnp.einsum("gqk,gkd->gqd", probs_low, values, preferred_element_type=F32)
    attended = group_merge(att_split, tokens).astype(BF)
    middle = source + dot(attended, out_t, 1, 1)
    second_scale = norm_scale(middle)
    normed2 = (middle * second_scale * gain2).astype(BF)

    normed2_all, ffn_all = exchange(4, (normed2, "col", "g"), (ffn_block, "row", "g"))
    normed2_all = normed2_all.reshape(cols * tokens, width)
    cot_all = cot_all.reshape(cols * tokens, width)
    ffn_all = ffn_all.reshape(width, 3 * hidden)
    gate_up = dot(normed2_all, ffn_all[:, : 2 * hidden])
    gate, up = gate_up[:, :hidden], gate_up[:, hidden:]
    down_t = ffn_all[:, 2 * hidden :]
    sigma = jax.nn.sigmoid(gate)
    active = (gate * sigma * up).astype(BF)
    d_active = dot(cot_all, down_t)
    d_gate = (d_active * up * sigma * (1.0 + gate * (1.0 - sigma))).astype(BF)
    d_up = (d_active * gate * sigma).astype(BF)
    d_gate_up = jnp.concatenate([d_gate, d_up], axis=1)
    d_second_part = dot(d_gate_up, ffn_all[:, : 2 * hidden], 1, 1).astype(BF)
    ffn_part = dot(active, down_t, 1, 1).astype(BF)
    ffn_grad = jnp.concatenate(
        [dot(normed2_all, d_gate_up, 0, 0), dot(cot_all, active, 0, 0)], axis=1
    ).astype(BF)
    d_second, ffn_rows = exchange(
        5,
        (d_second_part.reshape(cols, tokens, width), "col", "s"),
        (ffn_grad.reshape(rows, feat, 3 * hidden), "row", "s"),
    )
    d_second = jnp.sum(d_second.astype(F32), axis=0)
    ffn_sum = jnp.sum(ffn_rows.astype(F32), axis=0).astype(BF)

    second_back, gain2_grad = norm_back(middle, second_scale, gain2, d_second)
    d_middle = upstream + second_back
    d_attn = d_middle.astype(BF)
    d_attended = dot(d_attn, out_t).astype(BF)
    out_grad = dot(d_attn, attended, 0, 0)
    d_split = group_split(d_attended)
    row_dots = jnp.sum(d_split.astype(F32) * att_split, axis=2, keepdims=True)
    d_probs = jnp.einsum("gqd,gkd->gqk", d_split, values, preferred_element_type=F32)
    d_raw = (probs * (d_probs - row_dots) * soft_scale).astype(BF)
    d_query = group_merge(
        jnp.einsum("gqk,gkd->gqd", d_raw, keys, preferred_element_type=F32), tokens
    )
    d_key = jnp.einsum("gqk,gqd->kgd", d_raw, split_q, preferred_element_type=F32)
    d_value = jnp.einsum("gqk,gqd->kgd", probs_low, d_split, preferred_element_type=F32)
    d_kv = jnp.stack([d_key, d_value], axis=1).astype(BF)
    d_kv = d_kv.reshape(rows, cols * tokens, 2 * kv_width)
    d_kv_rows, ffn_out, ffn_dp = exchange(
        6,
        (d_kv, "row", "s"),
        (ffn_part.reshape(cols, tokens, width), "col", "s"),
        (ffn_sum, "dp", "g"),
    )
    d_kv_sum = jnp.sum(d_kv_rows.astype(F32), axis=0).astype(BF)
    result = (middle + jnp.sum(ffn_out.astype(F32), axis=0)).astype(BF)

    def by_row(own):
        return own.reshape(tokens, rows, feat).transpose(1, 0, 2)

    d_kv_cols, out_rows, result_rows = exchange(
        7,
        (d_kv_sum.reshape(cols, tokens, 2 * kv_width), "col", "s"),
        (out_grad.astype(BF).reshape(rows, feat, width), "row", "s"),
        (by_row(result), "row", "s"),
    )
    out_sum = jnp.sum(out_rows.astype(F32), axis=0).astype(BF)
    out_sum = out_sum.reshape(feat, cols, q_cols).transpose(1, 0, 2)
    d_kv_own = jnp.sum(d_kv_cols.astype(F32), axis=0)
    d_turned = rotate(jnp.concatenate([d_query, d_kv_own[:, :kv_width]], axis=1), cosine, -sine)
    d_qkv = jnp.concatenate([d_turned, d_kv_own[:, kv_width:]], axis=1).astype(BF)
    d_first = dot(d_qkv, qkv_weight, 1, 1)
    qkv_grad = dot(normed1, d_qkv, 0, 0)
    first_back, gain1_grad = norm_back(source, first_scale, gain1, d_first)
    input_grad_own = (d_middle + first_back).astype(BF)

    gain_grads = jnp.stack([gain1_grad, gain2_grad]).reshape(2, rows, feat).transpose(1, 0, 2)
    qkv_rows, gain_rows, input_rows, out_cols = exchange(
        8,
        (qkv_grad.astype(BF).reshape(rows, feat, width + 2 * kv_width), "row", "s"),
        (gain_grads, "row", "s"),
        (by_row(input_grad_own), "row", "s"),
        (out_sum, "col", "s"),
    )
    qkv_sum = jnp.sum(qkv_rows.astype(F32), axis=0).astype(BF)
    qkv_sum = jnp.concatenate(
        [
            qkv_sum[:, :width].reshape(feat, cols, q_cols),
            qkv_sum[:, width : width + kv_width].reshape(feat, cols, k_cols),
            qkv_sum[:, width + kv_width :].reshape(feat, cols, k_cols),
        ],
        axis=2,
    ).transpose(1, 0, 2)
    out_own = jnp.sum(out_cols.astype(F32), axis=0).astype(BF)
    qkv_cols, gain_cols, out_dp = exchange(
        9,
        (qkv_sum, "col", "s"),
        (jnp.sum(gain_rows, axis=0), "col", "g"),
        (out_own, "dp", "g"),
    )
    qkv_own = jnp.sum(qkv_cols.astype(F32), axis=0).astype(BF)
    qkv_dp, gain_dp = exchange(10, (qkv_own, "dp", "g"), (jnp.sum(gain_cols, axis=0), "dp", "g"))
    qkv_final = jnp.sum(qkv_dp.astype(F32), axis=0)
    out_final = jnp.sum(out_dp.astype(F32), axis=0)
    ffn_final = jnp.sum(ffn_dp.astype(F32), axis=0)
    gain_final = jnp.sum(gain_dp, axis=0)
    return (
        result_rows.reshape(block_tokens, feat),
        input_rows.reshape(block_tokens, feat),
        gain_final[0],
        qkv_final[:, :q_cols],
        qkv_final[:, q_cols : q_cols + k_cols],
        qkv_final[:, q_cols + k_cols :],
        out_final.T,
        gain_final[1],
        ffn_final[:, :hidden],
        ffn_final[:, hidden : 2 * hidden],
        ffn_final[:, 2 * hidden :].T,
    )


def solution(mesh):
    placed = (
        P(("dp", "col"), "row"),
        P("row"),
        P("row", "col"),
        P("row", "col"),
        P("row", "col"),
        P("col", "row"),
        P("row"),
        P("row", "col"),
        P("row", "col"),
        P("col", "row"),
        P(("dp", "col"), "row"),
    )
    return jax.shard_map(
        on_device,
        mesh=mesh,
        in_specs=placed,
        out_specs=(
            P(("dp", "col"), "row"),
            P(("dp", "col"), "row"),
            P("row"),
            P("row", "col"),
            P("row", "col"),
            P("row", "col"),
            P("col", "row"),
            P("row"),
            P("row", "col"),
            P("row", "col"),
            P("col", "row"),
        ),
        check_vma=False,
    )
```
